32 devices in a mesh: dp: 4 (over y, core), ep: 8 (over z, x).
Axes of the slice: x: 2, y: 2, z: 4, core: 2. Of those that a mesh axis runs over, the one named last changes fastest.
Arguments:
- tokens: bfloat16 [32, 256, 2048], P(('dp', 'ep')), may hold values from -6 to 6
- lengths: int32 [32], P(('dp', 'ep')), may hold values from 64 to 256, as said below
- routes: int32 [32, 256, 8], P(('dp', 'ep')), may hold values from 0 to 15, all different within a row
- pair_order: int32 [32, 2048], P(('dp', 'ep')), may hold values from 0 to 2047, each once within a row
- gate_weights: float32 [32, 256, 8], P(('dp', 'ep')), may hold values from 0.05 to 0.5
- attn_weight: bfloat16 [2048, 8192], P(('dp', 'ep')), may hold values from -0.375 to 0.375
- gains: float32 [4352], replicated, may hold values from 0.5 to 1.5
- expert_gate_up: bfloat16 [16, 2048, 2048], P('ep'), may hold values from -0.125 to 0.125
- expert_down: bfloat16 [16, 1024, 2048], P('ep'), may hold values from -0.375 to 0.375
- cotangent: bfloat16 [32, 256, 2048], P(('dp', 'ep')), may hold values from -6 to 6
Outputs:
- output: bfloat16 [32, 256, 2048], P(('dp', 'ep'))
- input_grad: float32 [32, 256, 2048], P(('dp', 'ep'))
- attn_weight_grad: float32 [2048, 8192], P(('dp', 'ep'))
- gains_grad: float32 [4352], P(('dp', 'ep'))
- gate_up_grad: float32 [16, 2048, 2048], P('ep', 'dp')
- down_grad: float32 [16, 1024, 2048], P('ep', 'dp')
The draws below stay inside these ranges and needn't reach their ends.
Inputs may be any that keep to these rules, and one draw needn't show every extreme that they name: `lengths`: slots at or beyond a sequence's length are padding; in every draw some sequence fills all 256 slots. `routes`: the 8 experts of a slot are distinct. `pair_order`: within each sequence every value appears once.
All inputs are finite; a program needn't handle non-finite values.
Results may differ from the reference program's by a relative error of at most 0.014.
Values may be sent and summed in bfloat16 or wider, within the bound.
No kernel may reach another device: no remote copies, remote signals or barrier semaphores. Data moves between devices by JAX's collectives and lax.ppermute only.
A program may use at most 448 MiB of HBM per device.

```python
import math
import jax
import jax.numpy as jnp
from jax import lax

D = 2048
HEADS = 16
HEAD = 128
FF = 1024
TOPK = 8
SLOTS = 256
EXPERTS = 16
SEQS = 32
CAP = 144


def draw_lengths(key, part):
    first_key, second_key = jax.random.split(key)
    drawn = jax.random.randint(first_key, (SEQS,), SLOTS // 4, SLOTS + 1)
    chosen = jax.random.randint(second_key, (), 0, SEQS)
    return jnp.where(jnp.arange(SEQS) == chosen, SLOTS, drawn).astype(jnp.int32)


def strengthened(values, stream_key, source, target, blocks, factor):
    owner, partner = [(jnp.arange(values.shape[dim]) // (values.shape[dim] // blocks)).reshape([-1 if axis == dim else 1 for axis in range(values.ndim)]) for dim in (source, target)]
    chosen = jax.random.permutation(stream_key, blocks)[partner]
    strong = (owner == chosen) | (owner == (partner + blocks // 2) % blocks)
    return jnp.where(strong, factor * values, values)


def levels(key, shape, cuts, least, high):
    def one(position, parts):
        heights = jax.random.uniform(jax.random.fold_in(jax.random.fold_in(key, 6), position), (parts,), jnp.float32, least / len(cuts), high / len(cuts))
        return jnp.repeat(jnp.exp(heights), shape[position] // parts).reshape((-1,) + (1,) * (len(shape) - position - 1))

    factor_of = one(*cuts[0])
    for cut in cuts[1:]:
        factor_of = factor_of * one(*cut)
    return factor_of


def different_ones(own_key, rows, count, top, lift):
    ranking = jax.random.permutation(jax.random.fold_in(own_key, 1), count)
    pull = ranking
    for power in range(3):
        pull = pull * pull // count
    pull = pull * lift // count
    chance = jax.random.randint(jax.random.fold_in(own_key, 2), (rows, count), 0, 4096) + pull
    holders = jax.random.permutation(jax.random.fold_in(own_key, 3), rows)[jnp.arange(count) % rows]
    chance = jnp.where(jnp.arange(rows)[:, None] == holders[None, :], 1 << 14, chance)
    priority = chance * count + jnp.arange(count)
    return lax.top_k(priority.astype(jnp.int32), top)[1].astype(jnp.int32)


def gaussian(stream_key, dims, spread, reach, shards=(), kind=jnp.bfloat16):
    values = spread * jax.random.normal(stream_key, dims, jnp.float32)
    if shards:
        values = values * levels(stream_key, dims, shards, -0.22, 0.18)
    return jnp.clip(values, -reach, reach).astype(kind)


def noise_with(key, shape, width, bound, shards, heavy, held_as=jnp.bfloat16):
    entries = width * jax.random.normal(key, shape, jnp.float32)
    if shards:
        entries = entries * levels(key, shape, shards, -0.22, 0.18)
    return jnp.clip(strengthened(entries, jax.random.fold_in(key, 3), *heavy), -bound, bound).astype(held_as)


def setup_inputs(seed: int = 0) -> dict:
    keys = jax.random.split(jax.random.key(seed), 11)
    tokens = noise_with(keys[0], (SEQS, SLOTS, D), 1.0, 6.0, ((0, 32),), (0, 2, 32, 2.75))
    lengths = draw_lengths(jax.random.fold_in(keys[10], 71), 0)
    routes = different_ones(keys[2], SEQS * SLOTS, EXPERTS, TOPK, 8192).reshape((SEQS, SLOTS, TOPK))
    pair_order = jax.vmap(lambda own: jax.random.permutation(own, SLOTS * TOPK))(jax.random.split(keys[3], SEQS)).reshape((SEQS, SLOTS * TOPK)).astype(jnp.int32)
    gate_weights = jnp.clip(jnp.exp(math.log(0.5) - 2.3025851 * jax.random.uniform(keys[4], (SEQS, SLOTS, TOPK), jnp.float32) ** levels(keys[4], (SEQS, SLOTS, TOPK), ((0, 32),), -0.2, 0.2)), 0.05, 0.5)
    attn_weight = gaussian(keys[5], (D, 4 * D), (D // 8) ** -0.5, 0.375, ((0, 32),))
    gains = jnp.clip(1.0 + 0.1 * jax.random.normal(keys[6], (2 * D + 2 * HEAD,), jnp.float32), 0.5, 1.5)
    expert_gate_up = gaussian(keys[7], (EXPERTS, D, 2 * FF), D ** -0.5, 0.125, ((0, 8),))
    expert_down = gaussian(keys[8], (EXPERTS, FF, D), (FF // 4) ** -0.5, 0.375, ((0, 8),))
    cotangent = gaussian(keys[9], (SEQS, SLOTS, D), 1.0, 6.0, ((0, 32),))
    return {"tokens": tokens, "lengths": lengths, "routes": routes, "pair_order": pair_order, "gate_weights": gate_weights, "attn_weight": attn_weight, "gains": gains, "expert_gate_up": expert_gate_up, "expert_down": expert_down, "cotangent": cotangent}


@jax.custom_vjp
def low(v):
    return lax.optimization_barrier(v.astype(jnp.bfloat16)).astype(jnp.float32)

@jax.custom_vjp
def low_back(v):
    return v

def low_keep(v):
    return (low(v), None)

def low_pass(kept, grad):
    return (grad,)

def back_keep(v):
    return (v, None)

def back_low(kept, grad):
    return (low(grad),)
low.defvjp(low_keep, low_pass)
low_back.defvjp(back_keep, back_low)
EPS = 1e-06
THETA = 10000.0
NEG = -1e+30
HIGHEST = lax.Precision.HIGHEST

def matmul(left, right):
    return jnp.dot(left, right, precision=HIGHEST, preferred_element_type=jnp.float32)

def rms_norm(values, gain_vec):
    return values * lax.rsqrt(lax.optimization_barrier(jnp.mean(values * values, axis=-1, keepdims=True)) + EPS) * gain_vec

def rope_tables(slot_count, head_size):
    half_size = head_size // 2
    frequency = THETA ** (-(jnp.arange(half_size, dtype=jnp.float32) * 2.0) / head_size)
    angles = jnp.arange(slot_count, dtype=jnp.float32)[:, None] * frequency[None, :]
    return (jnp.cos(angles)[:, None, :], jnp.sin(angles)[:, None, :])

def rotary(values, cosine_table, sine_table):
    half_size = values.shape[-1] // 2
    first_half = values[..., :half_size]
    second_half = values[..., half_size:]
    return jnp.concatenate([first_half * cosine_table - second_half * sine_table, second_half * cosine_table + first_half * sine_table], axis=-1)

def pair_slots(route_rows, order_row, length):
    pair_count = SLOTS * TOPK
    expert_flat = route_rows.reshape(pair_count).astype(jnp.int32)
    pair_index = jnp.arange(pair_count, dtype=jnp.int32)
    pair_live = pair_index // TOPK < length
    by_rank = jnp.zeros((pair_count,), jnp.int32).at[order_row].set(pair_index)
    one_hot = ((expert_flat[by_rank][:, None] == jnp.arange(EXPERTS, dtype=jnp.int32)[None, :]) & pair_live[by_rank][:, None]).astype(jnp.int32)
    earlier = jnp.cumsum(one_hot, axis=0) - one_hot
    pair_rank = lax.optimization_barrier(jnp.sum(earlier * one_hot, axis=1))[order_row]
    kept_pair = pair_live & (pair_rank < CAP)
    dest_slot = jnp.where(kept_pair, expert_flat * CAP + pair_rank, EXPERTS * CAP).astype(jnp.int32)
    return (dest_slot, kept_pair)

def layer_sequence(inputs, attn_full, gain_all, gate_up_w, down_w, route_rows, order_row, length, gate_row):
    gain_attn = gain_all[:D]
    gain_ffn = gain_all[D:2 * D]
    gain_query = gain_all[2 * D:2 * D + HEAD]
    gain_key = gain_all[2 * D + HEAD:]
    live_rows = (jnp.arange(SLOTS) < length).astype(jnp.float32)[:, None]
    xn_first = low(rms_norm(inputs, gain_attn))
    query_raw = low_back(matmul(xn_first, attn_full[:, :D])).reshape(SLOTS, HEADS, HEAD)
    key_raw = low_back(matmul(xn_first, attn_full[:, D:2 * D])).reshape(SLOTS, HEADS, HEAD)
    values = low(low_back(matmul(xn_first, attn_full[:, 2 * D:3 * D]))).reshape(SLOTS, HEADS, HEAD)
    cosine_table, sine_table = rope_tables(SLOTS, HEAD)
    query_rot = low(rotary(rms_norm(query_raw, gain_query), cosine_table, sine_table))
    key_rot = low(rotary(rms_norm(key_raw, gain_key), cosine_table, sine_table))
    factor = 1.0 / math.sqrt(HEAD)
    raw_scores = jnp.einsum('qhd,khd->hqk', query_rot, key_rot, precision=HIGHEST) * factor
    key_live = jnp.arange(SLOTS) < length
    scores = low_back(jnp.where(key_live[None, None, :], raw_scores, NEG))
    probs = jax.nn.softmax(scores, axis=-1)
    attended = jnp.einsum('hqk,khd->qhd', low(probs), values, precision=HIGHEST).reshape(SLOTS, D)
    attended = low(low_back(attended))
    resid = inputs + low_back(matmul(attended, attn_full[:, 3 * D:]))
    xn_second = low(rms_norm(resid, gain_ffn))
    dest_slot, kept_pair = pair_slots(route_rows, order_row, length)
    token_of = jnp.arange(SLOTS * TOPK, dtype=jnp.int32) // TOPK
    buffer = jnp.zeros((EXPERTS * CAP + 1, D), jnp.float32).at[dest_slot].set(xn_second[token_of])
    buffer = low_back(buffer[:EXPERTS * CAP].reshape(EXPERTS, CAP, D))
    gate_up = low_back(jnp.einsum('ecd,edf->ecf', buffer, gate_up_w, precision=HIGHEST))
    activation = low(jax.nn.silu(gate_up[..., :FF]) * gate_up[..., FF:])
    expert_out = low(low_back(jnp.einsum('ecf,efd->ecd', activation, down_w, precision=HIGHEST)))
    out_ext = jnp.concatenate([expert_out.reshape(EXPERTS * CAP, D), jnp.zeros((1, D), jnp.float32)], axis=0)
    weight = jnp.where(kept_pair, gate_row.reshape(SLOTS * TOPK), 0.0)
    mixed = lax.optimization_barrier(jnp.sum((out_ext[dest_slot] * weight[:, None]).reshape(SLOTS, TOPK, D), axis=1))
    return live_rows * (resid + mixed)

def reference(tokens, lengths, routes, pair_order, gate_weights, attn_weight, gains, expert_gate_up, expert_down, cotangent):
    inputs = tokens.astype(jnp.float32)
    attn_full = attn_weight.astype(jnp.float32)
    gate_up_w = expert_gate_up.astype(jnp.float32)
    down_w = expert_down.astype(jnp.float32)
    gain_all = gains.astype(jnp.float32)
    gate_rows = gate_weights.astype(jnp.float32)

    def forward(inputs, attn_full, gain_all, gate_up_w, down_w):

        def one_sequence(pieces):
            seq_in, route_rows, order_row, length, gate_row = pieces
            return layer_sequence(seq_in, attn_full, gain_all, gate_up_w, down_w, route_rows, order_row, length, gate_row)
        return lax.map(jax.checkpoint(one_sequence), (inputs, routes, pair_order, lengths, gate_rows))
    result, pullback = jax.vjp(forward, inputs, attn_full, gain_all, gate_up_w, down_w)
    grads = pullback(cotangent.astype(jnp.float32))
    return (result.astype(jnp.bfloat16), grads[0], grads[1], grads[2], grads[3], grads[4])
```

```python
import math

import jax
import jax.numpy as jnp
from jax import lax
from jax.sharding import PartitionSpec as P

HEAD = 128
EPS = 1e-06
THETA = 10000.0
NEG = -1e30
LOW = jnp.bfloat16
F32 = jnp.float32


def swap(value, axis, mask):
    count = lax.axis_size(axis)
    return lax.ppermute(value, axis, [(i, i ^ mask) for i in range(count)])


def gather_slots(shard, axis):
    slots = {0: shard}
    bit = lax.axis_size(axis) // 2
    while bit:
        for r in sorted(slots):
            slots[r | bit] = swap(slots[r], axis, bit)
        bit //= 2
    return [slots[r] for r in range(lax.axis_size(axis))]


def scatter_slots(parts, axis):
    acc = [part.astype(F32) for part in parts]
    bit = 1
    while bit < lax.axis_size(axis):
        for r in range(0, len(acc), 2 * bit):
            acc[r] = acc[r] + swap(acc[r | bit].astype(LOW), axis, bit).astype(F32)
        bit *= 2
    return acc[0]


def sum_all(value):
    for axis in ("ep", "dp"):
        bit = 1
        while bit < lax.axis_size(axis):
            value = value + swap(value, axis, bit)
            bit *= 2
    return value


def inv_rms(values):
    return lax.rsqrt(jnp.mean(values * values, axis=-1, keepdims=True) + EPS)


def norm_back(values, inv_scale, gain_vec, grad_in):
    scaled = grad_in * gain_vec
    mean_term = jnp.mean(scaled * values, axis=-1, keepdims=True)
    return inv_scale * scaled - values * (inv_scale * inv_scale * inv_scale) * mean_term


def rope_tables(slot_count, head_size):
    half_size = head_size // 2
    frequency = THETA ** (-(jnp.arange(half_size, dtype=F32) * 2.0) / head_size)
    angles = jnp.arange(slot_count, dtype=F32)[:, None] * frequency[None, :]
    return (jnp.cos(angles)[:, None, :], jnp.sin(angles)[:, None, :])


def rotary(values, cosine_table, sine_table):
    half_size = values.shape[-1] // 2
    first_half = values[..., :half_size]
    second_half = values[..., half_size:]
    return jnp.concatenate(
        [
            first_half * cosine_table - second_half * sine_table,
            second_half * cosine_table + first_half * sine_table,
        ],
        axis=-1,
    )


def dot(a, b):
    return jnp.dot(a, b, preferred_element_type=F32)


def on_device(
    tokens,
    lengths,
    routes,
    pair_order,
    gate_weights,
    attn_weight,
    gains,
    expert_gate_up,
    expert_down,
    cotangent,
):
    slot_count, width = tokens.shape[1:]
    top_count = routes.shape[2]
    experts_dev, hidden = expert_down.shape[:2]
    rows_dev = attn_weight.shape[0]
    n_dp, n_ep = lax.axis_size("dp"), lax.axis_size("ep")
    my_dp, my_ep = lax.axis_index("dp"), lax.axis_index("ep")
    experts = experts_dev * n_ep
    capacity = (9 * slot_count * top_count + 8 * experts - 1) // (8 * experts)
    heads_dev = width // HEAD // n_dp
    cols = heads_dev * HEAD
    factor = 1.0 / math.sqrt(HEAD)

    inputs = tokens[0].astype(F32)
    length = lengths[0]
    slot_index = jnp.arange(slot_count)
    slot_live = slot_index < length
    live_rows = slot_live.astype(F32)[:, None]
    gain_attn = gains[:width]
    gain_ffn = gains[width : 2 * width]
    gain_query = gains[2 * width : 2 * width + HEAD]
    gain_key = gains[2 * width + HEAD :]

    blocks = attn_weight[:, : 3 * width].reshape(rows_dev, 3, n_dp, cols)
    qkv_shard = jnp.zeros((n_dp, rows_dev, 3 * cols), LOW)
    for r in range(n_dp):
        piece = lax.dynamic_index_in_dim(blocks, my_dp ^ r, axis=2, keepdims=False)
        piece = piece.reshape(rows_dev, 3 * cols)
        piece = swap(piece, "dp", r) if r else piece
        qkv_shard = lax.dynamic_update_slice(qkv_shard, piece[None], (my_dp ^ r, 0, 0))
    weight_qkv = jnp.zeros((n_dp, n_ep, rows_dev, 3 * cols), LOW)
    for s, shard in enumerate(gather_slots(qkv_shard, "ep")):
        weight_qkv = lax.dynamic_update_slice(weight_qkv, shard[:, None], (0, my_ep ^ s, 0, 0))
    weight_qkv = weight_qkv.reshape(width, 3 * cols)
    weight_out = jnp.zeros((n_ep, rows_dev, width), LOW)
    for s, shard in enumerate(gather_slots(attn_weight[:, 3 * width :], "ep")):
        weight_out = lax.dynamic_update_slice(weight_out, shard[None], (my_ep ^ s, 0, 0))
    weight_out = weight_out.reshape(cols, width)

    named = routes[0][:, :, None] == jnp.arange(experts, dtype=jnp.int32)
    order = pair_order[0].reshape(slot_count, top_count)[:, :, None]
    order_of = jnp.sum(jnp.where(named, order, 0), axis=1).T
    weight_of = jnp.sum(jnp.where(named, gate_weights[0][:, :, None], 0.0), axis=1).T
    live_pair = jnp.any(named, axis=1).T & slot_live[None, :]
    earlier = live_pair[:, :, None] & (order_of[:, :, None] < order_of[:, None, :])
    pair_rank = jnp.sum(earlier.astype(jnp.int32), axis=1)
    kept = live_pair & (pair_rank < capacity)
    place = jnp.where(kept, pair_rank.astype(F32), -1.0)
    meta = jnp.stack([place, jnp.where(kept, weight_of, 0.0)])
    meta = jnp.stack(gather_slots(meta, "ep"))
    meta = lax.dynamic_slice_in_dim(meta, my_ep * experts_dev, experts_dev, axis=2)
    place_in, weight_in = meta[:, 0], meta[:, 1]
    seats = jnp.arange(capacity, dtype=F32)
    chosen = place_in[:, :, None, :] == seats[None, None, :, None]
    row_weight = jnp.sum(jnp.where(chosen, weight_in[:, :, None, :], 0.0), axis=-1)
    row_weight = row_weight.reshape(n_ep, experts_dev * capacity, 1)
    pick = chosen.astype(LOW).reshape(n_ep, experts_dev * capacity, slot_count)

    scale_first = inv_rms(inputs)
    xn_own = (inputs * scale_first * gain_attn).astype(LOW)
    xn_first = jnp.stack(gather_slots(xn_own, "dp"))
    lens = jnp.stack(gather_slots(lengths, "dp"))
    projected = dot(xn_first.reshape(n_dp * slot_count, width), weight_qkv)
    projected = projected.reshape(n_dp, slot_count, 3, heads_dev, HEAD)
    query_raw, key_raw = projected[:, :, 0], projected[:, :, 1]
    values_low = projected[:, :, 2].astype(LOW)
    cosine, sine = rope_tables(slot_count, HEAD)
    query_scale, key_scale = inv_rms(query_raw), inv_rms(key_raw)
    query_rot = rotary(query_raw * query_scale * gain_query, cosine, sine).astype(LOW)
    key_rot = rotary(key_raw * key_scale * gain_key, cosine, sine).astype(LOW)
    raw = jnp.einsum("sqhd,skhd->shqk", query_rot, key_rot, preferred_element_type=F32) * factor
    key_live = slot_index[None, :] < lens
    scores = jnp.where(key_live[:, None, None, :], raw, NEG)
    probs = jax.nn.softmax(scores, axis=-1)
    probs_low = probs.astype(LOW)
    attended = jnp.einsum("shqk,skhd->sqhd", probs_low, values_low, preferred_element_type=F32)
    attended = attended.reshape(n_dp * slot_count, cols).astype(LOW)
    branch = dot(attended, weight_out).astype(LOW).reshape(n_dp, slot_count, width)
    resid = inputs + scatter_slots(list(branch), "dp")
    scale_second = inv_rms(resid)
    xn_second = (resid * scale_second * gain_ffn).astype(LOW)

    rows = jnp.einsum(
        "sct,std->scd", pick, jnp.stack(gather_slots(xn_second, "ep")), preferred_element_type=F32
    )
    received = rows.astype(LOW).reshape(n_ep, experts_dev, capacity, width)
    gate_up = jnp.einsum("sjcd,jdf->sjcf", received, expert_gate_up, preferred_element_type=F32)
    gate_part, up_part = gate_up[..., :hidden], gate_up[..., hidden:]
    sigmoid_gate = jax.nn.sigmoid(gate_part)
    activation = (gate_part * sigmoid_gate * up_part).astype(LOW)
    result = jnp.einsum("sjcf,jfd->sjcd", activation, expert_down, preferred_element_type=F32)
    result = result.reshape(n_ep, experts_dev * capacity, width) * row_weight
    mixed = jnp.einsum("sct,scd->std", pick, result.astype(LOW), preferred_element_type=F32)
    mixed = scatter_slots(list(mixed.astype(LOW)), "ep")
    output = (live_rows * (resid + mixed)).astype(LOW)

    grad_out = cotangent[0].astype(F32) * live_rows
    grad_rows = jnp.einsum(
        "sct,std->scd", pick, jnp.stack(gather_slots(cotangent[0], "ep")), preferred_element_type=F32
    )
    grad_recv = (grad_rows * row_weight).astype(LOW).reshape(n_ep, experts_dev, capacity, width)
    grad_act = jnp.einsum("sjcd,jfd->sjcf", grad_recv, expert_down, preferred_element_type=F32)
    grad_gate = grad_act * up_part * sigmoid_gate * (1.0 + gate_part * (1.0 - sigmoid_gate))
    grad_up = grad_act * gate_part * sigmoid_gate
    grad_gate_up = jnp.concatenate([grad_gate, grad_up], axis=-1).astype(LOW)
    back = jnp.einsum("sjcf,jdf->sjcd", grad_gate_up, expert_gate_up, preferred_element_type=F32)
    back = back.astype(LOW).reshape(n_ep, experts_dev * capacity, width)
    back = jnp.einsum("sct,scd->std", pick, back, preferred_element_type=F32)
    grad_xn_second = scatter_slots(list(back.astype(LOW)), "ep")
    grad_down = jnp.einsum("sjcf,sjcd->jfd", activation, grad_recv, preferred_element_type=F32)
    grad_weight_gu = jnp.einsum("sjcd,sjcf->jdf", received, grad_gate_up, preferred_element_type=F32)

    def expert_sum(grad):
        part = grad.shape[1] // n_dp
        parts = grad.astype(LOW).reshape(experts_dev, n_dp, part, width)
        return scatter_slots(
            [lax.dynamic_index_in_dim(parts, my_dp ^ r, axis=1, keepdims=False) for r in range(n_dp)], "dp"
        )

    down_grad = expert_sum(grad_down)
    gate_up_grad = expert_sum(grad_weight_gu)

    grad_resid = grad_out + norm_back(resid, scale_second, gain_ffn, grad_xn_second)
    grad_gain_ffn = jnp.sum(grad_xn_second * resid * scale_second, axis=0)
    grad_branch = jnp.stack(gather_slots(grad_resid.astype(LOW), "dp"))
    grad_branch = grad_branch.reshape(n_dp * slot_count, width)
    grad_wout = jnp.einsum("sa,sb->ab", attended, grad_branch, preferred_element_type=F32)
    grad_att = jnp.einsum("sb,ab->sa", grad_branch, weight_out, preferred_element_type=F32)
    grad_att = grad_att.astype(LOW).reshape(n_dp, slot_count, heads_dev, HEAD)
    grad_probs = jnp.einsum("sqhd,skhd->shqk", grad_att, values_low, preferred_element_type=F32)
    grad_values = jnp.einsum("shqk,sqhd->skhd", probs_low, grad_att, preferred_element_type=F32)
    inner_sum = jnp.sum(probs * grad_probs, axis=-1, keepdims=True)
    grad_scores = (probs * (grad_probs - inner_sum)).astype(LOW)
    grad_qrot = jnp.einsum("shqk,skhd->sqhd", grad_scores, key_rot, preferred_element_type=F32) * factor
    grad_krot = jnp.einsum("shqk,sqhd->skhd", grad_scores, query_rot, preferred_element_type=F32) * factor
    grad_qnorm = rotary(grad_qrot, cosine, -sine)
    grad_knorm = rotary(grad_krot, cosine, -sine)
    grad_query = norm_back(query_raw, query_scale, gain_query, grad_qnorm).astype(LOW)
    grad_key = norm_back(key_raw, key_scale, gain_key, grad_knorm).astype(LOW)
    grad_gain_query = jnp.sum(grad_qnorm * query_raw * query_scale, axis=(0, 1, 2))
    grad_gain_key = jnp.sum(grad_knorm * key_raw * key_scale, axis=(0, 1, 2))
    grad_proj = jnp.stack([grad_query, grad_key, grad_values.astype(LOW)], axis=2)
    grad_proj = grad_proj.reshape(n_dp * slot_count, 3 * cols)
    grad_wqkv = jnp.einsum(
        "sa,sb->ab",
        xn_first.reshape(n_dp * slot_count, width),
        grad_proj,
        preferred_element_type=F32,
    )
    grad_xn_first = jnp.einsum("sb,ab->sa", grad_proj, weight_qkv, preferred_element_type=F32)
    grad_xn_first = grad_xn_first.astype(LOW).reshape(n_dp, slot_count, width)
    grad_xn_first = scatter_slots(list(grad_xn_first), "dp")
    input_grad = grad_resid + norm_back(inputs, scale_first, gain_attn, grad_xn_first)
    grad_gain_attn = jnp.sum(grad_xn_first * inputs * scale_first, axis=0)

    parts = grad_wqkv.astype(LOW).reshape(n_dp, n_ep, rows_dev, 3 * cols)
    share = scatter_slots(
        [lax.dynamic_index_in_dim(parts, my_ep ^ s, axis=1, keepdims=False) for s in range(n_ep)], "ep"
    )
    qkv_share = jnp.zeros((rows_dev, 3, n_dp, cols), F32)
    for r in range(n_dp):
        piece = lax.dynamic_index_in_dim(share, my_dp ^ r, axis=0, keepdims=False)
        piece = swap(piece.astype(LOW), "dp", r).astype(F32) if r else piece
        piece = piece.reshape(rows_dev, 3, 1, cols)
        qkv_share = lax.dynamic_update_slice(qkv_share, piece, (0, 0, my_dp ^ r, 0))
    parts = grad_wout.astype(LOW).reshape(n_ep, rows_dev, width)
    out_share = scatter_slots(
        [lax.dynamic_index_in_dim(parts, my_ep ^ s, axis=0, keepdims=False) for s in range(n_ep)], "ep"
    )
    attn_share = jnp.concatenate([qkv_share.reshape(rows_dev, 3 * width), out_share], axis=1)

    gain_terms = jnp.concatenate([grad_gain_attn, grad_gain_ffn, grad_gain_query, grad_gain_key])
    gain_part = gain_terms.shape[0] // (n_dp * n_ep)
    gain_share = lax.dynamic_slice_in_dim(
        sum_all(gain_terms), (my_dp * n_ep + my_ep) * gain_part, gain_part
    )
    return (output[None], input_grad[None], attn_share, gain_share, gate_up_grad, down_grad)


def solution(mesh):
    in_specs = (
        P(("dp", "ep"), None, None),
        P(("dp", "ep")),
        P(("dp", "ep"), None, None),
        P(("dp", "ep"), None),
        P(("dp", "ep"), None, None),
        P(("dp", "ep"), None),
        P(),
        P("ep", None, None),
        P("ep", None, None),
        P(("dp", "ep"), None, None),
    )
    out_specs = (
        P(("dp", "ep"), None, None),
        P(("dp", "ep"), None, None),
        P(("dp", "ep"), None),
        P(("dp", "ep")),
        P("ep", "dp", None),
        P("ep", "dp", None),
    )
    return jax.shard_map(
        on_device, mesh=mesh, in_specs=in_specs, out_specs=out_specs, check_vma=False
    )
```

```python
import functools
import math

import jax
import jax.numpy as jnp
from jax import lax
from jax.experimental import pallas as pl
from jax.experimental.pallas import tpu as pltpu
from jax.sharding import PartitionSpec as P

HEAD = 128
EPS = 1e-06
THETA = 10000.0
NEG = -1e30
LOW = jnp.bfloat16
F32 = jnp.float32
VMEM_LIMIT = 60 * 1024 * 1024


def swap(value, axis, mask):
    count = lax.axis_size(axis)
    return lax.ppermute(value, axis, [(i, i ^ mask) for i in range(count)])


def after(value, *others):
    return lax.optimization_barrier((value, *others))[0]


class Order:
    def __init__(self):
        self.last = None

    def __call__(self, *values):
        if self.last is not None:
            values = lax.optimization_barrier((*values, self.last))[:-1]
        self.last = values[0]
        return values if len(values) > 1 else values[0]

    def pin(self, value):
        return after(value, self.last)


class Gather:
    def __init__(self, order, shard, axis, gates=None):
        self.order, self.axis, self.got, self.gates = order, axis, {0: shard}, gates or {}
        count = lax.axis_size(axis)
        self.waiting = [1, 2, 4, 3, 6, 5, 7] if count == 8 else list(range(1, count))

    def take(self, count=None):
        ks, self.waiting = self.waiting[:count], self.waiting[count:] if count else []
        for k in ks:
            shard = self.got[k & (k - 1)]
            if k in self.gates:
                shard = after(shard, self.gates[k])
            self.got[k] = self.order(swap(shard, self.axis, k & -k))

    def take_to(self, k):
        self.take(self.waiting.index(k) + 1)

    def slots(self):
        return [self.got[k] for k in sorted(self.got)]

    def evens(self):
        return [self.got[k] for k in sorted(self.got) if k % 2 == 0]


def scatter_steps(r, top):
    bits = [1 << b for b in range(top.bit_length() - 1)]
    for bit in reversed(bits):
        yield from scatter_steps(r | bit, bit)
    for bit in bits:
        yield bit, r


class Scatter:
    def __init__(self, order, parts, axis, gates=None):
        self.order, self.axis, self.parts, self.gates = order, axis, list(parts), gates or {}
        self.waiting = list(scatter_steps(0, len(self.parts)))
        self.arrived = {}

    def take(self, count=None):
        steps, self.waiting = self.waiting[:count], self.waiting[count:] if count else []
        for bit, r in steps:
            sent = self.parts[r | bit].astype(LOW)
            before = self.arrived.setdefault(bit, [])
            if len(before) > 1:
                sent = after(sent, before[-2])
            if bit in self.gates:
                sent = after(sent, self.gates[bit])
            got = self.order(swap(sent, self.axis, bit))
            before.append(got)
            self.before, self.arrival = self.parts[r], got
            self.parts[r] = self.parts[r].astype(F32) + got.astype(F32)

    @property
    def total(self):
        return self.parts[0]


class Stack:
    def __init__(self, order, odd, even, axis, gates=None):
        self.order, self.axis, self.gates = order, axis, gates or {}
        self.bit, self.sent, self.terms = 1, odd, [(even, 1)]

    def take(self):
        gate = self.gates.get(self.bit)
        sent = self.sent if gate is None else after(self.sent, gate)
        got = self.order(swap(sent, self.axis, self.bit))
        self.bit, self.sent = 2 * self.bit, None
        self.terms.append((got, 1))
        if self.bit < lax.axis_size(self.axis):
            self.sent = sum(v[step :: 2 * step].astype(F32) for v, step in self.terms).astype(LOW)
            self.terms = [(v, 2 * step) for v, step in self.terms]

    def stacks(self):
        return [v for v, _ in self.terms]

    @property
    def total(self):
        return sum(v[0].astype(F32) for v in self.stacks())


class Sum:
    def __init__(self, order, value, axes):
        self.order, self.value = order, value
        self.waiting = [(a, 1 << b) for a in axes for b in range(lax.axis_size(a).bit_length() - 1)]

    def take(self, count=None):
        steps, self.waiting = self.waiting[:count], self.waiting[count:] if count else []
        for axis, bit in steps:
            self.value = self.value + self.order(swap(self.value, axis, bit))


def inv_rms(values):
    return lax.rsqrt(jnp.mean(values * values, axis=-1, keepdims=True) + EPS)


def norm_back(values, inv_scale, gain_vec, grad_in):
    scaled = grad_in * gain_vec
    mean_term = jnp.mean(scaled * values, axis=-1, keepdims=True)
    return inv_scale * scaled - values * (inv_scale * inv_scale * inv_scale) * mean_term


def rope_tables(slot_count):
    half_size = HEAD // 2
    frequency = THETA ** (-(jnp.arange(half_size, dtype=F32) * 2.0) / HEAD)
    angles = jnp.arange(slot_count, dtype=F32)[:, None] * frequency[None, :]
    cosine, sine = jnp.cos(angles), jnp.sin(angles)
    return jnp.concatenate([cosine, cosine], axis=1), jnp.concatenate([-sine, sine], axis=1)


def dot(a, b, contract=((1,), (0,))):
    return lax.dot_general(a, b, (contract, ((), ())), preferred_element_type=F32)


NT = ((1,), (1,))
TN = ((0,), (0,))


def call(kernel, grid, in_specs, out_specs, out_shape, flops, moved, scratch=(), prefetch=0, aliases=None):
    return pl.pallas_call(
        kernel,
        grid_spec=pltpu.PrefetchScalarGridSpec(
            num_scalar_prefetch=prefetch,
            grid=grid,
            in_specs=in_specs,
            out_specs=out_specs,
            scratch_shapes=list(scratch),
        ),
        out_shape=out_shape,
        input_output_aliases=aliases or {},
        compiler_params=pltpu.CompilerParams(vmem_limit_bytes=VMEM_LIMIT),
        cost_estimate=pl.CostEstimate(flops=flops, bytes_accessed=moved, transcendentals=0),
    )


def whole(dims):
    return pl.BlockSpec(dims, lambda *_: (0,) * len(dims), pipeline_mode=pl.Buffered(1))


def shape(dims, kind):
    return jax.ShapeDtypeStruct(dims, kind)


HBM = pl.BlockSpec(memory_space=pl.ANY)


def head_parts(raw, gain_vec, cosine, sine):
    scale = inv_rms(raw)
    normed = raw * scale * gain_vec
    rotated = normed * cosine + pltpu.roll(normed, HEAD // 2, axis=1) * sine
    return scale, rotated.astype(LOW)


def head_powers(query_rot, key_rot, values, length):
    scores = dot(query_rot, key_rot, NT)
    live = lax.broadcasted_iota(jnp.int32, scores.shape, 1) < length
    powers = jnp.where(live, jnp.exp(scores * (1.0 / math.sqrt(HEAD))), 0.0)
    sums = dot(powers.astype(LOW), jnp.concatenate([values, jnp.ones_like(values)], axis=1))
    inverse = 1.0 / sums[:, HEAD:]
    return powers, sums[:, :HEAD] * inverse, inverse


def attention_kernel(lens, xn, weight, gain, cosine, sine, proj, att, branch):
    length = lens[pl.program_id(0)]
    cols = att.shape[2]
    for part in range(3):
        proj[0, :, part * cols : (part + 1) * cols] = dot(xn[0], weight[:, part * cols : (part + 1) * cols])
    cos, sin = cosine[...], sine[...]
    for at in range(0, cols, HEAD):
        _, query_rot = head_parts(proj[0, :, at : at + HEAD], gain[0:1], cos, sin)
        _, key_rot = head_parts(proj[0, :, cols + at : cols + at + HEAD], gain[1:2], cos, sin)
        values = proj[0, :, 2 * cols + at : 2 * cols + at + HEAD].astype(LOW)
        att[0, :, at : at + HEAD] = head_powers(query_rot, key_rot, values, length)[1].astype(LOW)
    for c in range(branch.shape[2] // cols):
        block = weight[c * cols : (c + 1) * cols, 3 * cols :]
        branch[0, :, c * cols : (c + 1) * cols] = dot(att[0], block).astype(LOW)


def attention(lens, xn, weight, gain, cosine, sine):
    n_seq, slots, width = xn.shape
    cols = weight.shape[1] // 4
    one = lambda last: pl.BlockSpec((1, slots, last), lambda s, _: (s, 0, 0))
    return call(
        attention_kernel,
        (n_seq,),
        [one(width)] + [whole(v.shape) for v in (weight, gain, cosine, sine)],
        [one(3 * cols), one(cols), one(width)],
        [shape((n_seq, slots, 3 * cols), F32), shape((n_seq, slots, cols), LOW), shape(xn.shape, LOW)],
        flops=8 * n_seq * slots * width * cols,
        moved=weight.size * 2 + n_seq * slots * (4 * width + 14 * cols),
        prefetch=1,
    )(lens, xn, weight, gain, cosine, sine)


def attention_back_kernel(lens, grad, proj, xn, weight, gain, cosine, sine, grad_proj, grad_xn, grad_gain, grad_scaled):
    length = lens[pl.program_id(0)]
    cols = proj.shape[2] // 3
    factor = 1.0 / math.sqrt(HEAD)

    @pl.when(pl.program_id(0) == 0)
    def _():
        grad_gain[...] = jnp.zeros_like(grad_gain)
        grad_scaled[...] = jnp.zeros_like(grad_scaled)

    grad_att = jnp.zeros((grad.shape[1], cols), F32)
    for c in range(grad.shape[2] // cols):
        block = weight[c * cols : (c + 1) * cols, 3 * cols :]
        grad_att = grad_att + dot(grad[0, :, c * cols : (c + 1) * cols], block, NT)
    grad_att = grad_att.astype(LOW)
    cos, sin = cosine[...], sine[...]
    for at in range(0, cols, HEAD):
        query_raw = proj[0, :, at : at + HEAD]
        key_raw = proj[0, :, cols + at : cols + at + HEAD]
        query_scale, query_rot = head_parts(query_raw, gain[0:1], cos, sin)
        key_scale, key_rot = head_parts(key_raw, gain[1:2], cos, sin)
        values = proj[0, :, 2 * cols + at : 2 * cols + at + HEAD].astype(LOW)
        powers, attended, inverse = head_powers(query_rot, key_rot, values, length)
        probs = powers * jnp.concatenate([inverse] * (powers.shape[1] // HEAD), axis=1)
        grad_head = grad_att[:, at : at + HEAD]
        grad_probs = dot(grad_head, values, NT)
        grad_values = dot(probs.astype(LOW), grad_head, TN)
        inner = jnp.sum(attended * grad_head.astype(F32), axis=-1, keepdims=True)
        grad_scores = (probs * (grad_probs - inner)).astype(LOW)
        grad_qrot = dot(grad_scores, key_rot) * factor
        grad_krot = dot(grad_scores, query_rot, TN) * factor
        grad_qnorm = grad_qrot * cos - pltpu.roll(grad_qrot, HEAD // 2, axis=1) * sin
        grad_knorm = grad_krot * cos - pltpu.roll(grad_krot, HEAD // 2, axis=1) * sin
        grad_query = norm_back(query_raw, query_scale, gain[0:1], grad_qnorm)
        grad_key = norm_back(key_raw, key_scale, gain[1:2], grad_knorm)
        grad_gain[0:1] += jnp.sum(grad_qnorm * query_raw * query_scale, axis=0, keepdims=True)
        grad_gain[1:2] += jnp.sum(grad_knorm * key_raw * key_scale, axis=0, keepdims=True)
        for part, value in enumerate((grad_query, grad_key, grad_values)):
            grad_proj[0, :, part * cols + at : part * cols + at + HEAD] = value.astype(LOW)
    for c in range(grad_xn.shape[2] // cols):
        rows = slice(c * cols, (c + 1) * cols)
        block = dot(grad_proj[0], weight[rows, : 3 * cols], NT)
        grad_xn[0, :, rows] = block.astype(LOW)
        grad_scaled[0:1, rows] += jnp.sum(block * xn[0, :, rows].astype(F32), axis=0, keepdims=True)


def attention_back(lens, grad, proj, xn, weight, gain, cosine, sine):
    n_seq, slots, width = grad.shape
    cols = weight.shape[1] // 4
    one = lambda last: pl.BlockSpec((1, slots, last), lambda s, _: (s, 0, 0))
    return call(
        attention_back_kernel,
        (n_seq,),
        [one(width), one(3 * cols), one(width)] + [whole(v.shape) for v in (weight, gain, cosine, sine)],
        [one(3 * cols), one(width)] + [pl.BlockSpec((8, last), lambda s, _: (0, 0)) for last in (HEAD, width)],
        [
            shape((n_seq, slots, 3 * cols), LOW),
            shape(grad.shape, LOW),
            shape((8, HEAD), F32),
            shape((8, width), F32),
        ],
        flops=8 * n_seq * slots * width * cols,
        moved=weight.size * 2 + n_seq * slots * (6 * width + 18 * cols),
        prefetch=1,
    )(lens, grad, proj, xn, weight, gain, cosine, sine)


def attention_weight_kernel(me, xn, grad_proj, att, grad, out):
    first = dot(xn[...], grad_proj[...], TN)
    second = dot(att[...], grad[...], TN)
    n_ep, rows = out.shape[0], out.shape[2]
    for j in range(n_ep):
        out[me[0] ^ j, 0, :, : first.shape[1]] = first[j * rows : (j + 1) * rows].astype(LOW)
        out[me[0] ^ j, 0, :, first.shape[1] :] = second[j * rows : (j + 1) * rows].astype(LOW)


def attention_weight_grad(me, xn, grad_proj, att, grad, n_ep):
    rows, width = xn.shape
    cols = att.shape[1]
    n_dp = width // cols
    strip = pl.BlockSpec((rows, cols), lambda i, _: (0, i))
    out = (n_ep, n_dp, cols // n_ep, 4 * cols)
    return call(
        attention_weight_kernel,
        (n_dp,),
        [strip, whole(grad_proj.shape), whole(att.shape), strip],
        pl.BlockSpec((n_ep, 1, cols // n_ep, 4 * cols), lambda i, _: (0, i, 0, 0)),
        shape(out, LOW),
        flops=8 * rows * width * cols,
        moved=rows * (4 * width + 8 * cols) + 8 * width * cols,
        prefetch=1,
    )(me, xn, grad_proj, att, grad)


def place_kernel(me, share, *refs):
    *pieces, out = refs
    n_dp, rows, _ = share.shape
    cols = share.shape[2] // 4
    width = n_dp * cols
    for r in range(n_dp):
        block = me[0] ^ r
        piece = pieces[r - 1][...].astype(F32) if r else share[block, :, : 3 * cols]
        for part in range(3):
            at = pl.multiple_of(part * width + block * cols, HEAD)
            out[:, pl.ds(at, cols)] = piece[:, part * cols : (part + 1) * cols]
        out[:, 3 * width + r * cols : 3 * width + (r + 1) * cols] = share[r, :, 3 * cols :]


def place_share(me, share, pieces):
    n_dp, rows, last = share.shape
    out = (rows, n_dp * last)
    return call(
        place_kernel,
        (1,),
        [whole(share.shape)] + [whole(p.shape) for p in pieces],
        pl.BlockSpec(out, lambda *_: (0, 0)),
        shape(out, F32),
        flops=0,
        moved=share.size * 10,
        prefetch=1,
    )(me, share, *pieces)


def one_hot(places, seats, axis):
    experts, slots = places.shape if axis == 0 else places.shape[::-1]
    dims = (experts * seats, slots) if axis == 0 else (slots, experts * seats)
    index = lax.broadcasted_iota(jnp.int32, dims, axis).astype(F32)
    hit = None
    for e in range(experts):
        spot = places[e : e + 1] if axis == 0 else places[:, e : e + 1]
        hit = (index == spot) if hit is None else hit | (index == spot)
    return hit.astype(LOW)


def seat_weights(places, weights, seats):
    experts, slots = places.shape
    index = lax.broadcasted_iota(jnp.int32, (experts * seats, slots), 0).astype(F32)
    total = jnp.zeros(index.shape, F32)
    for e in range(experts):
        total = jnp.where(index == places[e : e + 1], weights[e : e + 1], total)
    return jnp.sum(total, axis=1, keepdims=True)


def picked(out, place, xs, seats, weights=None):
    for s, x in enumerate(xs):
        rows = dot(one_hot(place[s], seats, 0), x[...])
        if weights is not None:
            rows = rows * seat_weights(place[s], weights[s], seats)
        for e in range(out.shape[0]):
            out[e, s * seats : (s + 1) * seats] = rows[e * seats : (e + 1) * seats].astype(LOW)


STRIP = 256


def grad_in_kernel(n_xs, seats, place, weights, *refs):
    xs, (down, grad_rows, grad_act) = refs[:n_xs], refs[n_xs:]

    @pl.when(pl.program_id(0) == 0)
    def _():
        picked(grad_rows, place, xs, seats, weights)

    for e in range(down.shape[0]):
        grad_act[e] = dot(grad_rows[e], down[e], NT).astype(LOW)


def grad_in(seats, place, weights, xs, down):
    experts, hidden, width = down.shape
    rows = len(xs) * seats
    return call(
        functools.partial(grad_in_kernel, len(xs), seats),
        (hidden // STRIP,),
        [whole(place.shape), whole(weights.shape)]
        + [whole(x.shape) for x in xs]
        + [pl.BlockSpec((experts, STRIP, width), lambda n: (0, n, 0))],
        [
            pl.BlockSpec((experts, rows, width), lambda n: (0, 0, 0)),
            pl.BlockSpec((experts, rows, STRIP), lambda n: (0, 0, n)),
        ],
        [shape((experts, rows, width), LOW), shape((experts, rows, hidden), LOW)],
        flops=2 * experts * rows * width * (hidden + xs[0].shape[0]),
        moved=down.size * 2 + experts * rows * (width + hidden) * 2,
    )(place, weights, *xs, down)


def gate_up_kernel(n_xs, seats, place, *refs):
    xs, (gate_w, up_w, grad_act) = refs[:n_xs], refs[n_xs : n_xs + 3]
    rows, activation, grad_gu = refs[-3:]

    @pl.when(pl.program_id(0) == 0)
    def _():
        picked(rows, place, xs, seats)

    for e in range(gate_w.shape[0]):
        gate = dot(rows[e], gate_w[e])
        up = dot(rows[e], up_w[e])
        sigmoid = jax.nn.sigmoid(gate)
        silu = gate * sigmoid
        grad = grad_act[e].astype(F32)
        activation[e] = (silu * up).astype(LOW)
        grad_gu[e, 0] = (grad * up * sigmoid * (1.0 + gate * (1.0 - sigmoid))).astype(LOW)
        grad_gu[e, 1] = (grad * silu).astype(LOW)


def gate_up(group, total, seats, place, xs, weight, grad_act, kept):
    experts, width, both = weight.shape
    hidden = both // 2
    rows = len(xs) * seats
    steps = hidden // STRIP
    outs = [
        shape((experts, total, width), LOW),
        shape((experts, total, hidden), LOW),
        shape((experts, 2, total, hidden), LOW),
    ]
    n_in = 4 + len(xs)
    return call(
        functools.partial(gate_up_kernel, len(xs), seats),
        (steps,),
        [whole(place.shape)]
        + [whole(x.shape) for x in xs]
        + [
            pl.BlockSpec((experts, width, STRIP), lambda n: (0, 0, n)),
            pl.BlockSpec((experts, width, STRIP), lambda n: (0, 0, n + steps)),
            pl.BlockSpec((experts, rows, STRIP), lambda n: (0, group, n)),
        ]
        + [HBM] * len(kept),
        [
            pl.BlockSpec((experts, rows, width), lambda n: (0, group, 0)),
            pl.BlockSpec((experts, rows, STRIP), lambda n: (0, group, n)),
            pl.BlockSpec((experts, 2, rows, STRIP), lambda n: (0, 0, group, n)),
        ],
        outs,
        flops=2 * experts * rows * width * (both + xs[0].shape[0]),
        moved=weight.size * 2 + experts * rows * (width + 2 * both) * 2,
        aliases={n_in + i: i for i in range(len(kept))},
    )(place, *xs, weight, weight, grad_act, *kept)


def combine_kernel(seats, dest, place, weights, spots, rows, weight, *refs):
    outs, (block, hot, scale) = refs[:-3], refs[-3:]
    n_xs, experts = spots.shape[0], rows.shape[0]
    apply = len(rows.shape) == 3

    @pl.when(pl.program_id(0) == 0)
    def _():
        for s in range(n_xs):
            hot[s] = one_hot(spots[s], seats, 1)
            if apply:
                scale[s] = seat_weights(place[s], weights[s], seats)

    for e in range(experts):
        if apply:
            result = dot(rows[e], weight[e])
        else:
            depth = rows.shape[3]
            result = dot(rows[e, 0], weight[e, :, :depth], NT) + dot(rows[e, 1], weight[e, :, depth:], NT)
        for s in range(n_xs):
            part = result[s * seats : (s + 1) * seats]
            if apply:
                part = part * scale[s, e * seats : (e + 1) * seats]
            block[s, e * seats : (e + 1) * seats] = part.astype(LOW)
    for s, (out, i) in enumerate(dest):
        outs[out][i] = dot(hot[s], block[s]).astype(LOW)


def combine(group, seats, dest, place, weights, rows, weight):
    experts, depth = rows.shape[0], rows.shape[-1]
    n_xs, _, slots = place.shape
    n_rows, strip = n_xs * seats, 512
    if rows.ndim == 3:
        width = weight.shape[2]
        row_spec = pl.BlockSpec((experts, n_rows, depth), lambda n: (0, group, 0))
        weight_spec = pl.BlockSpec((experts, depth, strip), lambda n: (0, 0, n))
    else:
        width = weight.shape[1]
        row_spec = pl.BlockSpec((experts, 2, n_rows, depth), lambda n: (0, 0, group, 0))
        weight_spec = pl.BlockSpec((experts, strip, 2 * depth), lambda n: (0, n, 0))
    spots = place.transpose(0, 2, 1)
    counts = [sum(1 for out, _ in dest if out == i) for i in range(1 + max(out for out, _ in dest))]
    return call(
        functools.partial(combine_kernel, seats, dest),
        (width // strip,),
        [whole(place.shape), whole(weights.shape), whole(spots.shape), row_spec, weight_spec],
        [pl.BlockSpec((count, slots, strip), lambda n: (0, 0, n)) for count in counts],
        [shape((count, slots, width), LOW) for count in counts],
        flops=2 * experts * n_rows * width * (depth * (rows.ndim - 2) + slots),
        moved=weight.size * 2 + experts * n_rows * depth * (rows.ndim - 2) * 2 + n_xs * slots * width * 2,
        scratch=[
            pltpu.VMEM((n_xs, experts * seats, strip), LOW),
            pltpu.VMEM((n_xs, slots, experts * seats), LOW),
            pltpu.VMEM((n_xs, experts * seats, 1), F32),
        ],
    )(place, weights, spots, rows, weight)


def expert_grad_kernel(me, rows, grad_gu, activation, grad_rows, send, keep):
    first, hidden = rows.shape[2], grad_gu.shape[3]

    def fill(out):
        for part in range(2):
            out[0, :first, part * hidden : (part + 1) * hidden] = dot(rows[0], grad_gu[0, part], TN).astype(LOW)
        out[0, first:] = dot(activation[0], grad_rows[0], TN).astype(LOW)

    pl.when(pl.program_id(0) < pl.num_programs(0) // 2)(functools.partial(fill, send))
    pl.when(pl.program_id(0) >= pl.num_programs(0) // 2)(functools.partial(fill, keep))


def expert_grad(e, me, rows, grad_gu, activation, grad_rows, n_dp):
    n_rows, width = rows.shape[1:]
    hidden = activation.shape[2]
    first, second, half = width // n_dp, hidden // n_dp, n_dp // 2
    rank = lambda i: jnp.where(i < half, 2 * i + 1, 2 * (i - half))
    strip = lambda last: pl.BlockSpec((1, n_rows, last), lambda i, me: (e, 0, rank(i) ^ me[0]))
    one = lambda *dims: pl.BlockSpec((1, *dims), lambda i, me: (e,) + (0,) * len(dims), pipeline_mode=pl.Buffered(1))
    out = (first + second, width)
    return call(
        expert_grad_kernel,
        (n_dp,),
        [strip(first), one(2, n_rows, hidden), strip(second), one(n_rows, width)],
        [
            pl.BlockSpec((1, *out), lambda i, me: (jnp.minimum(i, half - 1), 0, 0)),
            pl.BlockSpec((1, *out), lambda i, me: (jnp.maximum(i - half, 0), 0, 0)),
        ],
        [shape((half, *out), LOW)] * 2,
        flops=2 * n_rows * width * 3 * hidden,
        moved=n_rows * (2 * width + 3 * hidden) * 2 + 3 * hidden * width * 2,
        prefetch=1,
    )(me, rows, grad_gu, activation, grad_rows)


def finish_kernel(n_terms, *refs):
    terms, (first, second) = refs[:n_terms], refs[-2:]
    rows = first.shape[1]
    total = terms[0][0].astype(F32)
    for term in terms[1:]:
        total = total + term[0].astype(F32)
    first[0] = total[:rows]
    second[0] = total[rows:]


def finish(e, experts, first, terms, kept):
    _, rows, width = terms[0].shape
    strip = 512
    outs = [shape((experts, first, width), F32), shape((experts, rows - first, width), F32)]
    return call(
        functools.partial(finish_kernel, len(terms)),
        (width // strip,),
        [pl.BlockSpec((1, rows, strip), lambda n: (0, 0, n))] * len(terms) + [HBM] * len(kept),
        [pl.BlockSpec((1, v.shape[1], strip), lambda n: (e, 0, n)) for v in outs],
        outs,
        flops=rows * width,
        moved=rows * width * (4 + 2 * len(terms)),
        aliases={len(terms) + i: i for i in range(len(kept))},
    )(*terms, *kept)


def on_device(
    tokens,
    lengths,
    routes,
    pair_order,
    gate_weights,
    attn_weight,
    gains,
    expert_gate_up,
    expert_down,
    cotangent,
):
    slot_count, width = tokens.shape[1:]
    top_count = routes.shape[2]
    experts_dev, hidden = expert_down.shape[:2]
    rows_dev = attn_weight.shape[0]
    n_dp, n_ep = lax.axis_size("dp"), lax.axis_size("ep")
    my_dp, my_ep = lax.axis_index("dp"), lax.axis_index("ep")
    at_dp, at_ep = my_dp.reshape(1), my_ep.reshape(1)
    experts = experts_dev * n_ep
    capacity = (9 * slot_count * top_count + 8 * experts - 1) // (8 * experts)
    seats = (capacity + 15) // 16 * 16
    cols = width // n_dp

    order = Order()
    inputs = tokens[0].astype(F32)
    length = lengths[0]
    gain_attn = gains[:width]
    gain_ffn = gains[width : 2 * width]
    gain_head = gains[2 * width :].reshape(2, HEAD)
    cosine, sine = rope_tables(slot_count)

    out_in = Gather(order, cotangent[0], "ep")
    out_in.take(2)

    slot_live = jnp.arange(slot_count) < length
    live_rows = slot_live.astype(F32)[:, None]
    named = routes[0][:, :, None] == jnp.arange(experts, dtype=jnp.int32)
    rank_of = pair_order[0].reshape(slot_count, top_count)[:, :, None]
    rank_of = jnp.sum(jnp.where(named, rank_of, 0), axis=1).T
    weight_of = jnp.sum(jnp.where(named, gate_weights[0][:, :, None], 0.0), axis=1).T
    live_pair = jnp.any(named, axis=1).T & slot_live[None, :]
    earlier = live_pair[:, :, None] & (rank_of[:, :, None] < rank_of[:, None, :])
    pair_rank = jnp.sum(earlier.astype(jnp.int32), axis=1)
    kept = live_pair & (pair_rank < capacity)
    place = jnp.where(kept, pair_rank.astype(F32), -1.0)
    weight_of = jnp.where(kept, weight_of, 0.0)
    weight_high = weight_of.astype(LOW)
    weight_low = (weight_of - weight_high.astype(F32)).astype(LOW)
    extra = jnp.concatenate([place.astype(LOW), weight_high, weight_low]).reshape(-1, 4 * cols)
    n_extra = extra.shape[0]
    extra = jnp.pad(extra, ((0, -n_extra % 16), (0, 0)))

    last = attn_weight[:, 3 * width :].reshape(rows_dev, n_dp, cols).transpose(1, 0, 2)
    shard = jnp.concatenate([jnp.zeros((n_dp, rows_dev, 3 * cols), LOW), last], axis=2)
    for r in reversed(range(n_dp)):
        block = my_dp ^ r
        piece = jnp.concatenate(
            [
                lax.dynamic_slice(attn_weight, (0, part * width + block * cols), (rows_dev, cols))
                for part in range(3)
            ],
            axis=1,
        )
        piece = swap(piece, "dp", r) if r else piece
        shard = lax.dynamic_update_slice(shard, piece[None], (block, 0, 0))
    shard = order(jnp.concatenate([shard.reshape(-1, 4 * cols), extra]))
    weights_in = Gather(order, shard, "ep")
    lens_in = Gather(order, order.pin(lengths), "dp")
    scale_first = inv_rms(inputs)
    xn_in = Gather(order, order.pin((inputs * scale_first * gain_attn).astype(LOW)), "dp")
    lens_in.take()
    xn_in.take(1)
    weights_in.take(2)
    xn_in.take(1)
    weights_in.take(2)
    xn_in.take()
    weights_in.take(n_ep - 6)
    out_in.gates = {4: order.last}
    weights_in.take(1)
    out_in.gates.update({k: order.last for k in out_in.waiting if k & (k - 1) == 2})
    weights_in.take()
    weight = jnp.zeros((n_dp, n_ep, rows_dev, 4 * cols), LOW)
    for s, part in sorted(weights_in.got.items()):
        part = part[: n_dp * rows_dev].reshape(n_dp, 1, rows_dev, 4 * cols)
        weight = lax.dynamic_update_slice(weight, part, (0, my_ep ^ s, 0, 0))
    weight = weight.reshape(width, 4 * cols)

    xn_first = jnp.stack(xn_in.slots())
    lens = order.pin(jnp.concatenate(lens_in.slots()))
    proj, attended, branch = order(*attention(lens, xn_first, weight, gain_head, cosine, sine))
    branch_sum = Scatter(order, list(branch), "dp")
    out_in.take_to(4)
    branch_sum.take(1)
    out_in.take(1)
    branch_sum.take()
    resid = inputs + branch_sum.total
    scale_second = inv_rms(resid)
    xn_second = order((resid * scale_second * gain_ffn).astype(LOW))

    x_in = Gather(order, xn_second, "ep")
    late = [n_ep - 3, n_ep - 1]
    early = [k for k in range(n_ep) if k not in late]
    ranked = early + late
    out_in.take(n_ep - 6)
    x_in.take(1)
    out_in.take()
    meta = jnp.stack([weights_in.got[k][n_dp * rows_dev :][:n_extra] for k in ranked])
    meta = meta.reshape(n_ep, 3, experts, slot_count).astype(F32)
    meta = lax.dynamic_slice_in_dim(meta, my_ep * experts_dev, experts_dev, axis=2)
    weight_in = meta[:, 1] + meta[:, 2]
    first_seat = jnp.arange(experts_dev, dtype=F32)[None, :, None] * seats
    place_in = jnp.where(meta[:, 0] < 0.0, -1.0, meta[:, 0] + first_seat)
    groups = [(0, slice(0, n_ep - 2), early), (n_ep // 2 - 1, slice(n_ep - 2, n_ep), late)]
    n_rows = n_ep * seats
    grad_rows, grad_act = order(
        *grad_in(seats, order.pin(place_in), weight_in, [out_in.got[k] for k in ranked], expert_down)
    )
    while any(k in x_in.waiting for k in early):
        x_in.take(1)
    backs = {}

    def forward_group(g, forward):
        at, h, ks = groups[g]
        xs = [x_in.got[k] for k in ks]
        return order(*gate_up(at, n_rows, seats, order.pin(place_in[h]), xs, expert_gate_up, grad_act, forward))

    def back_group(g):
        at, h, ks = groups[g]
        dest = [(i, 0) for i in range(len(ks))]
        terms = combine(at, seats, dest, order.pin(place_in[h]), weight_in[h], grad_gu, expert_gate_up)
        backs.update(zip(ks, [term[0] for term in order(*terms)], strict=True))

    forward = forward_group(0, [])
    x_in.take()
    rows, activation, grad_gu = forward_group(1, forward)
    back_group(1)
    back_group(0)
    back_sum = Scatter(order, [backs[k] for k in range(n_ep)], "ep")

    def expert_sum(e):
        terms = expert_grad(e, order.pin(at_dp), rows, grad_gu, activation, grad_rows, n_dp)
        return Stack(order, *order(*terms), "dp")

    back_sum.take(1)
    sums = [expert_sum(0)]
    back_sum.take(n_ep - 5)
    dest = [(1 - k % 2, k // 2) for k in ranked]
    mixes = order(*combine(0, seats, dest, order.pin(place_in), weight_in, activation, expert_down))
    back_sum.take(1)
    mixed = Stack(order, *mixes, "ep", {1: order.last})
    back_sum.take()
    grad_xn_second = back_sum.total

    grad_out = cotangent[0].astype(F32) * live_rows
    grad_resid = grad_out + norm_back(resid, scale_second, gain_ffn, grad_xn_second)
    grad_gain_ffn = jnp.sum(grad_xn_second * resid * scale_second, axis=0)
    grad_shard, grad_gain_ffn = order(grad_resid.astype(LOW), grad_gain_ffn)
    grad_in_dp = Gather(order, grad_shard, "dp")
    grad_in_dp.take(1)
    sums += [expert_sum(e) for e in range(1, experts_dev)]
    grad_in_dp.take()
    sums[0].take()
    sums[0].gates = {2: order.last}
    grad_branch = jnp.stack(grad_in_dp.slots())
    grad_proj, grad_xn, grad_gain_head, grad_scaled = order(
        *attention_back(order.pin(lens), grad_branch, proj, xn_first, weight, gain_head, cosine, sine)
    )
    grad_gain_attn = grad_scaled[0] / gain_attn
    gain_terms = jnp.concatenate([grad_gain_attn, grad_gain_ffn, grad_gain_head[0], grad_gain_head[1]])
    gain_sum = Sum(order, gain_terms, ("ep", "dp"))
    xn_sum = Scatter(order, list(grad_xn), "dp")
    xn_sum.take(1)
    flat = lambda v: v.reshape(n_dp * slot_count, -1)
    terms = order(
        attention_weight_grad(
            order.pin(at_ep), flat(xn_first), flat(grad_proj), flat(attended), flat(grad_branch), n_ep
        )
    )
    weight_sum = Scatter(order, list(terms), "ep")
    mixed.take()
    gain_sum.take(1)
    for total in sums[1:]:
        total.take()
    xn_sum.take()
    for total in sums[1:]:
        total.gates = {2: order.last}
    grad_xn_first = xn_sum.total
    input_grad = order(grad_resid + norm_back(inputs, scale_first, gain_attn, grad_xn_first))
    weight_sum.take(1)
    gain_sum.take(1)
    while mixed.sent is not None:
        mixed.take()
    output = order((live_rows * (resid + mixed.total)).astype(LOW))
    gain_sum.take(1)
    weight_sum.take(1)
    expert_grads = []
    for e, total in enumerate(sums):
        if e == len(sums) - 1:
            weight_sum.take(n_ep - 4)
            gain_sum.take()
            weight_sum.take()
            share = weight_sum.total
            pieces = []
            for r in range(1, n_dp):
                piece = lax.dynamic_index_in_dim(share, my_dp ^ r, axis=0, keepdims=False)
                pieces.append(swap(piece[:, : 3 * cols].astype(LOW), "dp", r))
        while total.sent is not None:
            total.take()
        expert_grads = order(*finish(e, experts_dev, width // n_dp, total.stacks(), expert_grads))
    gate_up_grad, down_grad = expert_grads
    attn_share = place_share(at_dp, share, pieces)
    gain_part = gain_terms.shape[0] // (n_dp * n_ep)
    gain_share = lax.dynamic_slice_in_dim(gain_sum.value, (my_dp * n_ep + my_ep) * gain_part, gain_part)
    return (output[None], input_grad[None], attn_share, gain_share, gate_up_grad, down_grad)


def solution(mesh):
    in_specs = (
        P(("dp", "ep"), None, None),
        P(("dp", "ep")),
        P(("dp", "ep"), None, None),
        P(("dp", "ep"), None),
        P(("dp", "ep"), None, None),
        P(("dp", "ep"), None),
        P(),
        P("ep", None, None),
        P("ep", None, None),
        P(("dp", "ep"), None, None),
    )
    out_specs = (
        P(("dp", "ep"), None, None),
        P(("dp", "ep"), None, None),
        P(("dp", "ep"), None),
        P(("dp", "ep")),
        P("ep", "dp", None),
        P("ep", "dp", None),
    )
    return jax.shard_map(
        on_device, mesh=mesh, in_specs=in_specs, out_specs=out_specs, check_vma=False
    )
```
